256 devices in a mesh: pipe: 4 (over y), fsdp: 32 (over x_hi, z, core), tensor: 2 (over x_lo).
Axes of the slice: x: 4 (x_hi: 2, x_lo: 2; x = x_hi * 2 + x_lo), y: 4, z: 8, core: 2. Of those that a mesh axis runs over, the one named last changes fastest.
Arguments:
- tokens: bfloat16 [6144, 4096], P('fsdp', 'tensor'), may hold values from -8 to 8
- norm_gains: float32 [4, 4096], P('pipe'), may hold values from 0.1 to 1.9
- q_blocks: bfloat16 [4, 4, 16, 256, 256], P('pipe', None, 'tensor', 'fsdp'), may hold values from -1 to 1
- k_blocks: bfloat16 [4, 4, 16, 256, 256], P('pipe', None, 'tensor', 'fsdp'), may hold values from -1 to 1
- v_blocks: bfloat16 [4, 4, 16, 256, 256], P('pipe', None, 'tensor', 'fsdp'), may hold values from -0.1875 to 0.1875
- o_blocks: bfloat16 [4, 4, 16, 256, 256], P('pipe', 'tensor', None, 'fsdp'), may hold values from -0.1875 to 0.1875
- q_rows: int32 [4, 4, 16], P('pipe', None, 'tensor'), may hold values from 0 to 15, as said below
- k_rows: int32 [4, 4, 16], P('pipe', None, 'tensor'), may hold values from 0 to 15, as said below
- v_rows: int32 [4, 4, 16], P('pipe', None, 'tensor'), may hold values from 0 to 15, as said below
- o_rows: int32 [4, 4, 16], P('pipe', 'tensor'), may hold values from 0 to 7, as said below
- mask_blocks: int32 [96, 4, 4], P('fsdp'), may hold values from 0 to 1, as said below
Outputs:
- activations: bfloat16 [4, 6144, 4096], P('pipe', 'fsdp', 'tensor')
The draws below stay inside these ranges and needn't reach their ends.
Inputs may be any that keep to these rules, and one draw needn't show every extreme that they name: `q_rows`: for each section and column block the 4 listed input blocks are distinct. `k_rows`: for each section and column block the 4 listed input blocks are distinct. `v_rows`: for each section and column block the 4 listed input blocks are distinct. `o_rows`: entries k and k2 with k // 2 == k2 // 2 name distinct head blocks of one column block. Every diagonal block mask_blocks[n, i, i] is 1.
All inputs are finite; a program needn't handle non-finite values.
Results may differ from the reference program's by a relative error of at most 0.017.
Values may be sent and summed in bfloat16 or wider, within the bound.
A program may use at most 64 MiB of HBM per device.

```python
import jax
import jax.numpy as jnp
from jax import lax

D = 4096
HEADS = 32
HD = 128
BS = 256
L = 64
MBLK = 16
SECTIONS = 4
TOKENS = 6144
SEQS = 96
LB = 4
KB = 16
PER = 4
HB = 16
HB_DEV = 8
OPER_T = 2
OPER = 4


def pick_distinct(base_key, groups, total, wanted):
    key_list = jax.random.split(base_key, groups)
    perm_rows = jax.vmap(lambda single: jax.random.permutation(single, total))(key_list)
    return perm_rows[:, :wanted]


def input_pattern(key, salt):
    chosen = pick_distinct(jax.random.fold_in(key, salt), SECTIONS * HB, KB, PER)
    return jnp.transpose(chosen.reshape(SECTIONS, HB, PER), (0, 2, 1)).astype(jnp.int32)


def draw_q_rows(key, part):
    return input_pattern(key, 11)


def draw_k_rows(key, part):
    return input_pattern(key, 12)


def draw_v_rows(key, part):
    return input_pattern(key, 13)


def draw_o_rows(key, part):
    halves = OPER // OPER_T
    chosen = pick_distinct(jax.random.fold_in(key, 14), SECTIONS * halves * KB, HB_DEV, OPER_T)
    shaped = chosen.reshape(SECTIONS, halves, KB, OPER_T)
    return jnp.transpose(shaped, (0, 1, 3, 2)).reshape(SECTIONS, OPER, KB).astype(jnp.int32)


def draw_mask_blocks(key, part):
    random_bits = jax.random.randint(jax.random.fold_in(key, 15), (SEQS, LB, LB), 0, 2)
    diagonal = (jnp.arange(LB)[:, None] == jnp.arange(LB)[None, :]).astype(jnp.int32)
    return jnp.maximum(random_bits, diagonal[None]).astype(jnp.int32)


def project_weights(key, salt):
    base_key = jax.random.fold_in(key, salt)
    shape = (SECTIONS, PER, HB, BS, BS)
    spread = (PER * BS) ** (-0.5)
    values = jnp.clip(jax.random.normal(base_key, shape, jnp.float32), -6.0, 6.0) * spread
    return values.astype(jnp.bfloat16)


def draw_q_blocks(key, part):
    return project_weights(key, 41)


def draw_k_blocks(key, part):
    return project_weights(key, 42)


def draw_tokens(key, part):
    base_key = jax.random.fold_in(key, 31)
    values = jnp.clip(jax.random.normal(base_key, (TOKENS, D), jnp.float32), -6.0, 6.0)
    return values.astype(jnp.bfloat16)


def levels(stream_key, dims, pieces, smallest, high):
    def one(dim, parts):
        draws = jax.random.uniform(jax.random.fold_in(jax.random.fold_in(stream_key, 6), dim), (parts,), jnp.float32, smallest / len(pieces), high / len(pieces))
        return jnp.repeat(jnp.exp(draws), dims[dim] // parts).reshape((-1,) + (1,) * (len(dims) - dim - 1))

    gain = one(*pieces[0])
    for cut in pieces[1:]:
        gain = gain * one(*cut)
    return gain


def normal_values(own_key, extent, scale, limit, cuts=(), kind=jnp.bfloat16):
    values = jax.random.normal(own_key, extent, jnp.float32) * scale
    if len(cuts) > 0:
        values = levels(own_key, extent, cuts, -0.22, 0.18) * values
    return jnp.clip(values, min=-limit, max=limit).astype(kind)


def setup_inputs(seed: int = 0) -> dict:
    streams_of = jax.random.split(jax.random.key(seed), 12)
    tokens = draw_tokens(jax.random.fold_in(streams_of[11], 71), 0)
    norm_gains = jnp.clip(1.0 + 0.18 * jax.random.normal(streams_of[1], (SECTIONS, D), jnp.float32), 0.1, 1.9)
    q_blocks = draw_q_blocks(jax.random.fold_in(streams_of[11], 71), 0)
    k_blocks = draw_k_blocks(jax.random.fold_in(streams_of[11], 71), 0)
    v_blocks = normal_values(streams_of[4], (SECTIONS, PER, HB, BS, BS), (PER * BS) ** -0.5, 0.1875, ((0, 4), (2, 2), (3, 32)))
    o_blocks = normal_values(streams_of[5], (SECTIONS, OPER, KB, BS, BS), (OPER * BS) ** -0.5, 0.1875, ((0, 4), (1, 2), (3, 32)))
    q_rows = draw_q_rows(jax.random.fold_in(streams_of[11], 71), 0)
    k_rows = draw_k_rows(jax.random.fold_in(streams_of[11], 71), 0)
    v_rows = draw_v_rows(jax.random.fold_in(streams_of[11], 71), 0)
    o_rows = draw_o_rows(jax.random.fold_in(streams_of[11], 71), 0)
    mask_blocks = draw_mask_blocks(jax.random.fold_in(streams_of[11], 71), 0)
    return dict(tokens=tokens, norm_gains=norm_gains, q_blocks=q_blocks, k_blocks=k_blocks, v_blocks=v_blocks, o_blocks=o_blocks, q_rows=q_rows, k_rows=k_rows, v_rows=v_rows, o_rows=o_rows, mask_blocks=mask_blocks)


def rms_rows(in_rows, gain_row):
    values = in_rows.astype(jnp.float32)
    inv_rms = lax.rsqrt(lax.optimization_barrier(jnp.mean(values * values, axis=-1, keepdims=True)) + 1e-05)
    return (values * inv_rms * gain_row.astype(jnp.float32)).astype(jnp.bfloat16)

def block_project(in_rows, blocks, pattern):
    row_count = in_rows.shape[0]
    block_width = blocks.shape[-1]
    row_blocks = in_rows.reshape(row_count, -1, block_width)
    picked = row_blocks[:, pattern]
    product = jnp.einsum('rpcb,pcbe->rce', picked.astype(jnp.float32), blocks.astype(jnp.float32))
    return product.reshape(row_count, -1)

def attend(queries, keys_proj, values_proj, mask_now):
    seq_count = mask_now.shape[0]
    head_shape = (seq_count, L, HEADS, HD)
    scores = jnp.einsum('sqhd,skhd->shqk', queries.reshape(head_shape).astype(jnp.float32), keys_proj.reshape(head_shape).astype(jnp.float32)) * HD ** (-0.5)
    allowed = jnp.repeat(jnp.repeat(mask_now, MBLK, axis=1), MBLK, axis=2) == 1
    scores = jnp.where(allowed[:, None], scores, jnp.float32(-1e+30))
    row_max = lax.optimization_barrier(jnp.max(scores, axis=-1, keepdims=True))
    exp_scores = jnp.exp(scores - row_max)
    probs = (exp_scores / lax.optimization_barrier(jnp.sum(exp_scores, axis=-1, keepdims=True))).astype(jnp.bfloat16)
    attended = jnp.einsum('shqk,skhd->sqhd', probs.astype(jnp.float32), values_proj.reshape(head_shape).astype(jnp.float32))
    return attended.astype(jnp.bfloat16).reshape(seq_count * L, HEADS * HD)

def reference(tokens, norm_gains, q_blocks, k_blocks, v_blocks, o_blocks, q_rows, k_rows, v_rows, o_rows, mask_blocks):
    current = tokens
    outputs = []
    tensor_group = jnp.arange(OPER, dtype=jnp.int32) // OPER_T
    for section in range(SECTIONS):
        normed = rms_rows(current, norm_gains[section])
        queries = block_project(normed, q_blocks[section], q_rows[section]).astype(jnp.bfloat16)
        keys_proj = block_project(normed, k_blocks[section], k_rows[section]).astype(jnp.bfloat16)
        values_proj = block_project(normed, v_blocks[section], v_rows[section]).astype(jnp.bfloat16)
        attended = attend(queries, keys_proj, values_proj, mask_blocks)
        full_rows = (o_rows[section] + tensor_group[:, None] * HB_DEV).astype(jnp.int32)
        branch = block_project(attended, o_blocks[section], full_rows)
        current = (current.astype(jnp.float32) + branch).astype(jnp.bfloat16)
        outputs.append(current)
    return jnp.stack(outputs)
```

```python
import functools

import jax
import jax.numpy as jnp
from jax import lax
from jax.experimental import pallas as pl
from jax.experimental.pallas import tpu as pltpu
from jax.sharding import PartitionSpec as P

HD = 128
MBLK = 16
MESH = pl.DeviceIdType.MESH
MATS = 4
BS = 256
UNIT = 16
LATE = (3,)


def kernel(
    sizes, tok, gain, q, k, v, o, q_rows, k_rows, v_rows, o_rows, mask, out,
    weights, raw, u_buf, normed, att, own, rs_send, rs_recv,
    cx_send, cx_recv, xe_send, xe_recv, xl_send, xl_recv, z_send, z_recv, cf_send, cf_recv,
    tk_send, tk_recv, rs_ssem, rs_rsem, u_ssem, u_rsem,
):
    nz, samples, seq = sizes
    pipe = lax.axis_index("pipe")
    fsdp = lax.axis_index("fsdp")
    t = lax.axis_index("tensor")
    pipes = lax.axis_size("pipe")
    core = lax.rem(fsdp, 2)
    z = lax.rem(fsdp // 2, nz)
    h = fsdp // (2 * nz)
    mate = fsdp + 1 - 2 * core

    def at_fsdp(hh, zz):
        return (hh * nz + zz) * 2 + core

    across = at_fsdp(1 - h, z)
    up = at_fsdp(h, lax.rem(z + 1, nz))
    down = at_fsdp(h, lax.rem(z + nz - 1, nz))
    previous = lax.rem(pipe + pipes - 1, pipes)

    barrier = pltpu.get_barrier_semaphore()
    for target in (mate, across, up, down):
        pl.semaphore_signal(barrier, inc=1, device_id={"fsdp": target}, device_id_type=MESH)
    pl.semaphore_signal(barrier, inc=1, device_id={"tensor": 1 - t}, device_id_type=MESH)
    for other in (t, 1 - t):
        pl.semaphore_signal(
            barrier, inc=1, device_id={"pipe": previous, "tensor": other}, device_id_type=MESH
        )
    pl.semaphore_wait(barrier, 7)

    shards = (q, k, v, o)
    halves = shards[0].shape[0] // 2
    mine = pl.ds(core * halves, halves)
    theirs = pl.ds((1 - core) * halves, halves)

    def remote(src, dst, ssem, rsem, device):
        return pltpu.make_async_remote_copy(
            src_ref=src, dst_ref=dst, send_sem=ssem, recv_sem=rsem, device_id=device,
            device_id_type=MESH,
        )

    swaps = []
    for mat in range(MATS):
        copy = remote(
            shards[mat].at[theirs], raw.at[mat], cx_send.at[mat], cx_recv.at[mat], {"fsdp": mate}
        )
        copy.start()
        swaps.append(copy)

    half_blocks = tok.shape[1] // BS

    def token_copy(b):
        return remote(
            tok.at[:, pl.ds(b * BS, BS)], u_buf.at[t * half_blocks + b], tk_send.at[b],
            tk_recv.at[b], {"tensor": 1 - t},
        )

    @pl.when(pipe == 0)
    def _():
        for b in range(half_blocks):
            token_copy(b).start()
        for b in range(half_blocks):
            u_buf[t * half_blocks + b] = tok[:, b * BS : (b + 1) * BS]

    def rows_of(hh, zz):
        return pl.ds(pl.multiple_of((hh * nz + zz) * UNIT, UNIT), UNIT)

    def piece(mat, hh, zz):
        return weights.at[mat, mine, rows_of(hh, zz)]

    def z_copy(way, slot, mat, step, hh, zz):
        target = up if way == 0 else down
        return remote(
            piece(mat, hh, zz), piece(mat, hh, zz), z_send.at[way, mat],
            z_recv.at[way, slot, mat, step], {"fsdp": target},
        )

    def core_copy(mat, hh, zz):
        return remote(
            piece(mat, hh, zz), piece(mat, hh, zz), cf_send.at[mat], cf_recv.at[mat],
            {"fsdp": mate},
        )

    def early_copy(mat):
        return remote(
            piece(mat, h, z), piece(mat, h, z), xe_send.at[mat], xe_recv.at[mat],
            {"fsdp": across},
        )

    def late_copy(mat, slot, hh, zz):
        return remote(
            piece(mat, hh, zz), piece(mat, hh, zz), xl_send.at[mat], xl_recv.at[mat, slot],
            {"fsdp": across},
        )

    def steps_of(way, mat):
        long = nz // 2
        return long if (mat % 2 == way) else nz - 1 - long

    for mat in range(MATS):
        swaps[mat].wait_recv()

        def join(i, carry, mat=mat):
            low = shards[mat][core * halves + i]
            high = raw[mat, i]
            first = jnp.where(core == 0, low, high)
            second = jnp.where(core == 0, high, low)
            weights[mat, core * halves + i, rows_of(h, z), :] = jnp.concatenate(
                [first, second], axis=0
            )
            return carry

        lax.fori_loop(0, halves, join, 0)
        if mat not in LATE:
            early_copy(mat).start()
        for way in range(2):
            z_copy(way, 0, mat, 0, h, z).start()
        core_copy(mat, h, z).start()
        if mat in LATE:
            late_copy(mat, 0, h, z).start()
    for mat in range(MATS):
        if mat in LATE:
            continue
        pltpu.make_async_copy(piece(mat, 1 - h, z), piece(mat, 1 - h, z), xe_recv.at[mat]).wait()
        for way in range(2):
            z_copy(way, 1, mat, 0, 1 - h, z).start()
        core_copy(mat, 1 - h, z).start()

    def got(ref, sem):
        pltpu.make_async_copy(ref, ref, sem).wait()

    late_queue = [(mat, 0, z) for mat in LATE]

    def drain_late(entries):
        for mat, slot, zz in entries:
            got(piece(mat, 1 - h, zz), xl_recv.at[mat, slot])
            core_copy(mat, 1 - h, zz).start()

    for step in range(nz // 2):
        pending, late_queue = late_queue, []
        for mat in range(MATS):
            for slot in range(1 if mat in LATE else 2):
                hh = h if slot == 0 else 1 - h
                for way in range(2):
                    if step >= steps_of(way, mat):
                        continue
                    if way == 0:
                        zz = lax.rem(z + nz - step - 1, nz)
                    else:
                        zz = lax.rem(z + step + 1, nz)
                    got(piece(mat, hh, zz), z_recv.at[way, slot, mat, step])
                    if step + 1 < steps_of(way, mat):
                        z_copy(way, slot, mat, step + 1, hh, zz).start()
                    core_copy(mat, hh, zz).start()
                    if mat in LATE:
                        place = 1 + step + way * steps_of(0, mat)
                        late_copy(mat, place, hh, zz).start()
                        late_queue.append((mat, place, zz))
        drain_late(pending)
    drain_late(late_queue)

    full = weights.shape[2]
    for mat in range(MATS):
        got(weights.at[mat, theirs], cf_recv.at[mat])

    @pl.when(pipe == 0)
    def _():
        for b in range(half_blocks):
            token_copy(b).wait()

    lanes = lax.broadcasted_iota(jnp.int32, (seq, seq), 1) // MBLK
    sublanes = lax.broadcasted_iota(jnp.int32, (seq, seq), 0) // MBLK
    mask_blocks = seq // MBLK
    all_blocks = 2 * half_blocks
    per = q_rows.shape[0]
    columns = q_rows.shape[1]
    chunks = 2
    chunk = half_blocks // chunks
    nt = (((1,), (1,)), ((), ()))

    def rs_copy(m, j, rows):
        where = pl.ds(j * chunk, chunk)
        return remote(
            rs_send.at[where, rows], rs_recv.at[where, rows], rs_ssem.at[m, j], rs_rsem.at[m, j],
            {"tensor": 1 - t},
        )

    def u_copy(m, j, rows, side):
        target = t if side == 0 else 1 - t
        return remote(
            out.at[pl.ds(j * chunk, chunk), rows],
            u_buf.at[pl.ds(t * half_blocks + j * chunk, chunk), rows],
            u_ssem.at[m, j, side], u_rsem.at[m, j, side],
            {"pipe": lax.rem(pipe + 1, pipes), "tensor": target},
        )

    def sample(m, carry):
        rows = pl.ds(pl.multiple_of(m * seq, seq), seq)

        @pl.when(pipe > 0)
        def _():
            for j in range(chunks):
                for side in range(2):
                    source = t if side == 0 else 1 - t
                    got(
                        u_buf.at[pl.ds(source * half_blocks + j * chunk, chunk), rows],
                        u_rsem.at[m, j, side],
                    )

        total = jnp.zeros((seq, BS), jnp.float32)
        for b in range(all_blocks):
            values = u_buf[b, rows, :].astype(jnp.float32)
            total = total + values * values
        mean = jnp.sum(total, axis=-1, keepdims=True) * (1.0 / (all_blocks * BS))
        inv_rms = lax.rsqrt(mean + 1e-05)
        for b in range(all_blocks):
            values = u_buf[b, rows, :].astype(jnp.float32)
            normed[b] = (values * inv_rms * gain[:, b * BS : (b + 1) * BS]).astype(jnp.bfloat16)

        allowed = jnp.zeros((seq, seq), jnp.int32)
        for i in range(mask_blocks):
            for jj in range(mask_blocks):
                here = (sublanes == i) & (lanes == jj)
                allowed = jnp.where(here, mask[m, i, jj], allowed)

        def project(mat, table, c):
            acc = None
            for p in range(per):
                term = jnp.dot(
                    normed[table[p, c]], weights[mat, p * columns + c],
                    preferred_element_type=jnp.float32,
                )
                acc = term if acc is None else acc + term
            return acc.astype(jnp.bfloat16)

        def column(c, inner):
            queries = project(0, q_rows, c)
            keys = project(1, k_rows, c)
            values = project(2, v_rows, c)
            for head in range(BS // HD):
                cut = slice(head * HD, (head + 1) * HD)
                scores = lax.dot_general(
                    queries[:, cut], keys[:, cut], nt, preferred_element_type=jnp.float32
                ) * HD ** (-0.5)
                scores = jnp.where(allowed == 1, scores, jnp.float32(-1e30))
                top = jnp.max(scores, axis=-1, keepdims=True)
                exps = jnp.exp(scores - top)
                probs = (exps / jnp.sum(exps, axis=-1, keepdims=True)).astype(jnp.bfloat16)
                att[c, :, cut] = jnp.dot(
                    probs, values[:, cut], preferred_element_type=jnp.float32
                ).astype(jnp.bfloat16)
            return inner

        lax.fori_loop(0, columns, column, 0, unroll=2)

        picks = o_rows.shape[0]

        def out_column(c):
            acc = None
            for p in range(picks):
                term = jnp.dot(
                    att[o_rows[p, c]], weights[3, p * all_blocks + c],
                    preferred_element_type=jnp.float32,
                )
                acc = term if acc is None else acc + term
            return acc

        for j in range(chunks):
            def away(i, inner):
                rs_send[i, rows, :] = out_column((1 - t) * half_blocks + i).astype(jnp.bfloat16)
                return inner

            lax.fori_loop(j * chunk, (j + 1) * chunk, away, 0, unroll=4)
            rs_copy(m, j, rows).start()

        def home(i, inner):
            own[i] = out_column(t * half_blocks + i)
            return inner

        lax.fori_loop(0, half_blocks, home, 0, unroll=4)
        for j in range(chunks):
            rs_copy(m, j, rows).wait_recv()
            for i in range(j * chunk, (j + 1) * chunk):
                base = u_buf[t * half_blocks + i, rows, :].astype(jnp.float32)
                branch = own[i] + rs_recv[i, rows, :].astype(jnp.float32)
                out[i, rows, :] = (base + branch).astype(jnp.bfloat16)

            @pl.when(pipe < pipes - 1)
            def _(j=j):
                for side in range(2):
                    u_copy(m, j, rows, side).start()

        return carry

    lax.fori_loop(0, samples, sample, 0)

    def drain(m, carry):
        rows = pl.ds(pl.multiple_of(m * seq, seq), seq)
        for j in range(chunks):
            rs_copy(m, j, rows).wait_send()

            @pl.when(pipe < pipes - 1)
            def _(j=j):
                for side in range(2):
                    u_copy(m, j, rows, side).wait_send()

        return carry

    lax.fori_loop(0, samples, drain, 0)
    for mat in range(MATS):
        swaps[mat].wait_send()
        got(weights.at[mat, mine], cf_send.at[mat])
        count = 1 if mat in LATE else 2
        for way in range(2):
            got(
                weights.at[mat, mine, pl.ds(0, UNIT * count * steps_of(way, mat))],
                z_send.at[way, mat],
            )
        if mat in LATE:
            got(weights.at[mat, mine, pl.ds(0, UNIT * nz)], xl_send.at[mat])
        else:
            got(piece(mat, h, z), xe_send.at[mat])


def body(
    tokens, norm_gains, q_blocks, k_blocks, v_blocks, o_blocks, q_rows, k_rows, v_rows, o_rows,
    mask_blocks,
):
    samples = mask_blocks.shape[0]
    row_count, half_width = tokens.shape
    seq = row_count // samples
    half = half_width // BS
    nz = lax.axis_size("fsdp") // 4
    shards = [
        w.reshape(-1, w.shape[-2], w.shape[-1]) for w in (q_blocks, k_blocks, v_blocks, o_blocks)
    ]
    blocks, depth, _ = shards[0].shape
    vmem = pl.BlockSpec(memory_space=pltpu.VMEM)
    smem = pl.BlockSpec(memory_space=pltpu.SMEM)
    dma = pltpu.SemaphoreType.DMA
    result = pl.pallas_call(
        functools.partial(kernel, (nz, samples, seq)),
        out_shape=jax.ShapeDtypeStruct((half, row_count, BS), jnp.bfloat16),
        in_specs=[vmem] * 6 + [smem] * 5,
        out_specs=vmem,
        scratch_shapes=[
            pltpu.VMEM((MATS, blocks, BS, BS), jnp.bfloat16),
            pltpu.VMEM((MATS, blocks // 2, depth, BS), jnp.bfloat16),
            pltpu.VMEM((2 * half, row_count, BS), jnp.bfloat16),
            pltpu.VMEM((2 * half, seq, BS), jnp.bfloat16),
            pltpu.VMEM((half, seq, BS), jnp.bfloat16),
            pltpu.VMEM((half, seq, BS), jnp.float32),
            pltpu.VMEM((half, row_count, BS), jnp.bfloat16),
            pltpu.VMEM((half, row_count, BS), jnp.bfloat16),
            dma((MATS,)),
            dma((MATS,)),
            dma((MATS,)),
            dma((MATS,)),
            dma((MATS,)),
            dma((MATS, nz)),
            dma((2, MATS)),
            dma((2, 2, MATS, nz // 2)),
            dma((MATS,)),
            dma((MATS,)),
            dma((half,)),
            dma((half,)),
            dma((samples, 2)),
            dma((samples, 2)),
            dma((samples, 2, 2)),
            dma((samples, 2, 2)),
        ],
        compiler_params=pltpu.CompilerParams(
            collective_id=0, has_side_effects=True, vmem_limit_bytes=48 << 20
        ),
    )(
        tokens, norm_gains, *shards, q_rows[0], k_rows[0], v_rows[0], o_rows[0], mask_blocks
    )
    return jnp.transpose(result, (1, 0, 2)).reshape(1, row_count, half_width)


def solution(mesh):
    placed = (
        P("fsdp", "tensor"),
        P("pipe", None),
        P("pipe", None, "tensor", "fsdp", None),
        P("pipe", None, "tensor", "fsdp", None),
        P("pipe", None, "tensor", "fsdp", None),
        P("pipe", "tensor", None, "fsdp", None),
        P("pipe", None, "tensor"),
        P("pipe", None, "tensor"),
        P("pipe", None, "tensor"),
        P("pipe", "tensor", None),
        P("fsdp", None, None),
    )
    return jax.shard_map(
        body, mesh=mesh, in_specs=placed, out_specs=P("pipe", "fsdp", "tensor"), check_vma=False
    )
```

```python
import functools

import jax
import jax.numpy as jnp
from jax import lax
from jax.experimental import pallas as pl
from jax.experimental.pallas import tpu as pltpu
from jax.sharding import PartitionSpec as P

HD = 128
MBLK = 16
MESH = pl.DeviceIdType.MESH
MATS = 4
BS = 256
UNIT = 16
LATE = (0, 1)
UNROLL_P = 2
UNROLL_A = 4


def kernel(
    sizes, tok, gain, q, k, v, o, q_rows, k_rows, v_rows, o_rows, mask, out,
    weights, raw, near, u_buf, normed, heads, att, own, rs_send, rs_recv, near_sem,
    cx_send, cx_recv, xe_send, xe_recv, xl_send, xl_recv, z_send, z_recv, cf_send, cf_recv,
    tk_send, tk_recv, own_sem, rs_ssem, rs_rsem, u_ssem, u_rsem,
):
    nz, samples, seq = sizes
    pipe = lax.axis_index("pipe")
    fsdp = lax.axis_index("fsdp")
    t = lax.axis_index("tensor")
    pipes = lax.axis_size("pipe")
    core = lax.rem(fsdp, 2)
    z = lax.rem(fsdp // 2, nz)
    h = fsdp // (2 * nz)
    mate = fsdp + 1 - 2 * core

    def at_fsdp(hh, zz):
        return (hh * nz + zz) * 2 + core

    across = at_fsdp(1 - h, z)
    up = at_fsdp(h, lax.rem(z + 1, nz))
    down = at_fsdp(h, lax.rem(z + nz - 1, nz))
    previous = lax.rem(pipe + pipes - 1, pipes)

    barrier = pltpu.get_barrier_semaphore()
    for target in (mate, across, up, down):
        pl.semaphore_signal(barrier, inc=1, device_id={"fsdp": target}, device_id_type=MESH)
    pl.semaphore_signal(barrier, inc=1, device_id={"tensor": 1 - t}, device_id_type=MESH)
    for other in (t, 1 - t):
        pl.semaphore_signal(
            barrier, inc=1, device_id={"pipe": previous, "tensor": other}, device_id_type=MESH
        )
    pl.semaphore_wait(barrier, 7)

    shards = (q, k, v, o)
    halves = shards[0].shape[0] // 2
    mine = pl.ds(core * halves, halves)
    theirs = pl.ds((1 - core) * halves, halves)

    def remote(src, dst, ssem, rsem, device):
        return pltpu.make_async_remote_copy(
            src_ref=src, dst_ref=dst, send_sem=ssem, recv_sem=rsem, device_id=device,
            device_id_type=MESH,
        )

    swaps = []
    for mat in range(MATS):
        copy = remote(
            shards[mat].at[theirs], raw.at[mat], cx_send.at[mat], cx_recv.at[mat], {"fsdp": mate}
        )
        copy.start()
        swaps.append(copy)
        pltpu.make_async_copy(shards[mat].at[mine], near.at[mat], near_sem.at[mat]).start()

    half_blocks = tok.shape[1] // BS

    def sample_rows(m):
        return pl.ds(pl.multiple_of(m * seq, seq), seq)

    def token_copy(m, b):
        return remote(
            tok.at[sample_rows(m), pl.ds(b * BS, BS)], u_buf.at[t * half_blocks + b, sample_rows(m)],
            tk_send.at[m], tk_recv.at[m], {"tensor": 1 - t},
        )

    def token_local(b):
        return pltpu.make_async_copy(
            tok.at[:, pl.ds(b * BS, BS)], u_buf.at[t * half_blocks + b], own_sem.at[b]
        )

    def send_tokens(first, last):
        @pl.when(pipe == 0)
        def _():
            for m in range(first, last):
                for b in range(half_blocks):
                    token_copy(m, b).start()

    def rows_of(hh, zz):
        return pl.ds(pl.multiple_of((hh * nz + zz) * UNIT, UNIT), UNIT)

    def piece(mat, hh, zz):
        return weights.at[mat, mine, rows_of(hh, zz)]

    def z_copy(way, slot, mat, step, hh, zz):
        target = up if way == 0 else down
        return remote(
            piece(mat, hh, zz), piece(mat, hh, zz), z_send.at[way, mat],
            z_recv.at[way, slot, mat, step], {"fsdp": target},
        )

    def core_copy(mat, hh, zz):
        return remote(
            piece(mat, hh, zz), piece(mat, hh, zz), cf_send.at[mat], cf_recv.at[mat],
            {"fsdp": mate},
        )

    def early_copy(mat):
        return remote(
            piece(mat, h, z), piece(mat, h, z), xe_send.at[mat], xe_recv.at[mat],
            {"fsdp": across},
        )

    def late_copy(mat, slot, hh, zz):
        return remote(
            piece(mat, hh, zz), piece(mat, hh, zz), xl_send.at[mat], xl_recv.at[mat, slot],
            {"fsdp": across},
        )

    def steps_of(way, mat):
        long = nz // 2
        return long if (mat % 2 == way) else nz - 1 - long

    for mat in range(MATS):
        swaps[mat].wait_recv()
        pltpu.make_async_copy(shards[mat].at[mine], near.at[mat], near_sem.at[mat]).wait()

        def join(i, carry, mat=mat):
            low = near[mat, i]
            high = raw[mat, i]
            first = jnp.where(core == 0, low, high)
            second = jnp.where(core == 0, high, low)
            weights[mat, core * halves + i, rows_of(h, z), :] = jnp.concatenate(
                [first, second], axis=0
            )
            return carry

        lax.fori_loop(0, halves, join, 0, unroll=4)
        if mat not in LATE:
            early_copy(mat).start()
        for way in range(2):
            z_copy(way, 0, mat, 0, h, z).start()
        core_copy(mat, h, z).start()
        if mat in LATE:
            late_copy(mat, 0, h, z).start()
    send_tokens(0, 1)

    @pl.when(pipe == 0)
    def _():
        for b in range(half_blocks):
            token_local(b).start()

    for mat in range(MATS):
        if mat in LATE:
            continue
        pltpu.make_async_copy(piece(mat, 1 - h, z), piece(mat, 1 - h, z), xe_recv.at[mat]).wait()
        for way in range(2):
            z_copy(way, 1, mat, 0, 1 - h, z).start()
        core_copy(mat, 1 - h, z).start()

    def got(ref, sem):
        pltpu.make_async_copy(ref, ref, sem).wait()

    late_queue = [(mat, 0, z) for mat in LATE]

    def drain_late(entries):
        for mat, slot, zz in entries:
            got(piece(mat, 1 - h, zz), xl_recv.at[mat, slot])
            core_copy(mat, 1 - h, zz).start()

    for step in range(nz // 2):
        pending, late_queue = late_queue, []
        for mat in range(MATS):
            for slot in range(1 if mat in LATE else 2):
                hh = h if slot == 0 else 1 - h
                for way in range(2):
                    if step >= steps_of(way, mat):
                        continue
                    if way == 0:
                        zz = lax.rem(z + nz - step - 1, nz)
                    else:
                        zz = lax.rem(z + step + 1, nz)
                    got(piece(mat, hh, zz), z_recv.at[way, slot, mat, step])
                    if step + 1 < steps_of(way, mat):
                        z_copy(way, slot, mat, step + 1, hh, zz).start()
                    core_copy(mat, hh, zz).start()
                    if mat in LATE:
                        place = 1 + step + way * steps_of(0, mat)
                        late_copy(mat, place, hh, zz).start()
                        late_queue.append((mat, place, zz))
        drain_late(pending)
    send_tokens(1, samples)
    drain_late(late_queue)

    full = weights.shape[2]
    for mat in range(MATS):
        got(weights.at[mat, theirs], cf_recv.at[mat])

    @pl.when(pipe == 0)
    def _():
        for b in range(half_blocks):
            token_local(b).wait()

    pair = BS // HD
    query_block = lax.rem(lax.broadcasted_iota(jnp.int32, (seq, pair * seq), 1), seq) // MBLK
    key_block = lax.broadcasted_iota(jnp.int32, (seq, pair * seq), 0) // MBLK
    mask_blocks = seq // MBLK
    all_blocks = 2 * half_blocks
    per = q_rows.shape[0]
    columns = q_rows.shape[1]
    chunks = 2
    chunk = half_blocks // chunks
    nt = (((1,), (1,)), ((), ()))

    def rs_copy(m, j, rows):
        where = pl.ds(j * chunk, chunk)
        return remote(
            rs_send.at[where, rows], rs_recv.at[where, rows], rs_ssem.at[m, j], rs_rsem.at[m, j],
            {"tensor": 1 - t},
        )

    def u_copy(m, j, rows, side):
        target = t if side == 0 else 1 - t
        return remote(
            out.at[pl.ds(j * chunk, chunk), rows],
            u_buf.at[pl.ds(t * half_blocks + j * chunk, chunk), rows],
            u_ssem.at[m, j, side], u_rsem.at[m, j, side],
            {"pipe": lax.rem(pipe + 1, pipes), "tensor": target},
        )

    def sample(m, carry):
        rows = sample_rows(m)

        @pl.when(pipe == 0)
        def _():
            got(u_buf.at[pl.ds((1 - t) * half_blocks, half_blocks), rows], tk_recv.at[m])

        @pl.when(pipe > 0)
        def _():
            for j in range(chunks):
                for side in range(2):
                    source = t if side == 0 else 1 - t
                    got(
                        u_buf.at[pl.ds(source * half_blocks + j * chunk, chunk), rows],
                        u_rsem.at[m, j, side],
                    )

        total = jnp.zeros((seq, BS), jnp.float32)
        for b in range(all_blocks):
            values = u_buf[b, rows, :].astype(jnp.float32)
            total = total + values * values
        mean = jnp.sum(total, axis=-1, keepdims=True) * (1.0 / (all_blocks * BS))
        inv_rms = lax.rsqrt(mean + 1e-05)
        for b in range(all_blocks):
            values = u_buf[b, rows, :].astype(jnp.float32)
            normed[b] = (values * inv_rms * gain[:, b * BS : (b + 1) * BS]).astype(jnp.bfloat16)

        allowed = jnp.zeros((seq, pair * seq), jnp.int32)
        for i in range(mask_blocks):
            for jj in range(mask_blocks):
                here = (query_block == i) & (key_block == jj)
                allowed = jnp.where(here, mask[m, i, jj], allowed)

        def project(mat, table, c):
            acc = None
            for p in range(per):
                term = jnp.dot(
                    normed[table[p, c]], weights[mat, p * columns + c],
                    preferred_element_type=jnp.float32,
                )
                acc = term if acc is None else acc + term
            return acc.astype(jnp.bfloat16)

        def column(c, inner):
            for mat, table in enumerate((q_rows, k_rows, v_rows)):
                heads[mat, c] = project(mat, table, c)
            return inner

        lax.fori_loop(0, columns, column, 0, unroll=UNROLL_P)

        def attend(c, inner):
            queries, keys, values = heads[0, c], heads[1, c], heads[2, c]
            empty = jnp.zeros((seq, HD), jnp.bfloat16)
            spread = jnp.concatenate(
                [
                    jnp.concatenate([queries[:, :HD], empty], axis=1),
                    jnp.concatenate([empty, queries[:, HD:]], axis=1),
                ],
                axis=0,
            )
            scores = lax.dot_general(
                keys, spread, nt, preferred_element_type=jnp.float32
            ) * HD ** (-0.5)
            scores = jnp.where(allowed == 1, scores, jnp.float32(-1e30))
            top = jnp.max(scores, axis=0, keepdims=True)
            exps = jnp.exp(scores - top)
            probs = (exps / jnp.sum(exps, axis=0, keepdims=True)).astype(jnp.bfloat16)
            mixed = lax.dot_general(
                probs, values, (((0,), (0,)), ((), ())), preferred_element_type=jnp.float32
            ).astype(jnp.bfloat16)
            att[c] = jnp.concatenate([mixed[:seq, :HD], mixed[seq:, HD:]], axis=1)
            return inner

        lax.fori_loop(0, columns, attend, 0, unroll=UNROLL_A)

        picks = o_rows.shape[0]

        def out_column(c):
            acc = None
            for p in range(picks):
                term = jnp.dot(
                    att[o_rows[p, c]], weights[3, p * all_blocks + c],
                    preferred_element_type=jnp.float32,
                )
                acc = term if acc is None else acc + term
            return acc

        for j in range(chunks):
            def away(i, inner):
                rs_send[i, rows, :] = out_column((1 - t) * half_blocks + i).astype(jnp.bfloat16)
                return inner

            lax.fori_loop(j * chunk, (j + 1) * chunk, away, 0, unroll=4)
            rs_copy(m, j, rows).start()

        def home(i, inner):
            own[i] = out_column(t * half_blocks + i)
            return inner

        lax.fori_loop(0, half_blocks, home, 0, unroll=4)
        for j in range(chunks):
            rs_copy(m, j, rows).wait_recv()
            for i in range(j * chunk, (j + 1) * chunk):
                base = u_buf[t * half_blocks + i, rows, :].astype(jnp.float32)
                branch = own[i] + rs_recv[i, rows, :].astype(jnp.float32)
                out[i, rows, :] = (base + branch).astype(jnp.bfloat16)

            @pl.when(pipe < pipes - 1)
            def _(j=j):
                for side in range(2):
                    u_copy(m, j, rows, side).start()

        return carry

    lax.fori_loop(0, samples, sample, 0)

    def drain(m, carry):
        rows = sample_rows(m)

        @pl.when(pipe == 0)
        def _():
            got(u_buf.at[pl.ds(t * half_blocks, half_blocks), rows], tk_send.at[m])

        for j in range(chunks):
            rs_copy(m, j, rows).wait_send()

            @pl.when(pipe < pipes - 1)
            def _(j=j):
                for side in range(2):
                    u_copy(m, j, rows, side).wait_send()

        return carry

    lax.fori_loop(0, samples, drain, 0)
    for mat in range(MATS):
        swaps[mat].wait_send()
        got(weights.at[mat, mine], cf_send.at[mat])
        count = 1 if mat in LATE else 2
        for way in range(2):
            got(
                weights.at[mat, mine, pl.ds(0, UNIT * count * steps_of(way, mat))],
                z_send.at[way, mat],
            )
        if mat in LATE:
            got(weights.at[mat, mine, pl.ds(0, UNIT * nz)], xl_send.at[mat])
        else:
            got(piece(mat, h, z), xe_send.at[mat])


def body(
    tokens, norm_gains, q_blocks, k_blocks, v_blocks, o_blocks, q_rows, k_rows, v_rows, o_rows,
    mask_blocks,
):
    samples = mask_blocks.shape[0]
    row_count, half_width = tokens.shape
    seq = row_count // samples
    half = half_width // BS
    nz = lax.axis_size("fsdp") // 4
    shards = [
        w.reshape(-1, w.shape[-2], w.shape[-1]) for w in (q_blocks, k_blocks, v_blocks, o_blocks)
    ]
    blocks, depth, _ = shards[0].shape
    vmem = pl.BlockSpec(memory_space=pltpu.VMEM)
    hbm = pl.BlockSpec(memory_space=pl.ANY)
    smem = pl.BlockSpec(memory_space=pltpu.SMEM)
    dma = pltpu.SemaphoreType.DMA
    result = pl.pallas_call(
        functools.partial(kernel, (nz, samples, seq)),
        out_shape=jax.ShapeDtypeStruct((half, row_count, BS), jnp.bfloat16),
        in_specs=[hbm, vmem] + [hbm] * 4 + [smem] * 5,
        out_specs=vmem,
        scratch_shapes=[
            pltpu.VMEM((MATS, blocks, BS, BS), jnp.bfloat16),
            pltpu.VMEM((MATS, blocks // 2, depth, BS), jnp.bfloat16),
            pltpu.VMEM((MATS, blocks // 2, depth, BS), jnp.bfloat16),
            pltpu.VMEM((2 * half, row_count, BS), jnp.bfloat16),
            pltpu.VMEM((2 * half, seq, BS), jnp.bfloat16),
            pltpu.VMEM((3, half, seq, BS), jnp.bfloat16),
            pltpu.VMEM((half, seq, BS), jnp.bfloat16),
            pltpu.VMEM((half, seq, BS), jnp.float32),
            pltpu.VMEM((half, row_count, BS), jnp.bfloat16),
            pltpu.VMEM((half, row_count, BS), jnp.bfloat16),
            dma((MATS,)),
            dma((MATS,)),
            dma((MATS,)),
            dma((MATS,)),
            dma((MATS,)),
            dma((MATS,)),
            dma((MATS, nz)),
            dma((2, MATS)),
            dma((2, 2, MATS, nz // 2)),
            dma((MATS,)),
            dma((MATS,)),
            dma((samples,)),
            dma((samples,)),
            dma((half,)),
            dma((samples, 2)),
            dma((samples, 2)),
            dma((samples, 2, 2)),
            dma((samples, 2, 2)),
        ],
        compiler_params=pltpu.CompilerParams(
            collective_id=0, has_side_effects=True, vmem_limit_bytes=48 << 20
        ),
    )(
        tokens, norm_gains, *shards, q_rows[0], k_rows[0], v_rows[0], o_rows[0], mask_blocks
    )
    return jnp.transpose(result, (1, 0, 2)).reshape(1, row_count, half_width)


def solution(mesh):
    placed = (
        P("fsdp", "tensor"),
        P("pipe", None),
        P("pipe", None, "tensor", "fsdp", None),
        P("pipe", None, "tensor", "fsdp", None),
        P("pipe", None, "tensor", "fsdp", None),
        P("pipe", "tensor", None, "fsdp", None),
        P("pipe", None, "tensor"),
        P("pipe", None, "tensor"),
        P("pipe", None, "tensor"),
        P("pipe", "tensor", None),
        P("fsdp", None, None),
    )
    return jax.shard_map(
        body, mesh=mesh, in_specs=placed, out_specs=P("pipe", "fsdp", "tensor"), check_vma=False
    )
```
